32 devices in a mesh: jown: 4 (over y, core), pown: 8 (over z, x).
Axes of the slice: x: 2, y: 2, z: 4, core: 2. Of those that a mesh axis runs over, the one named last changes fastest.
Arguments:
- vertex: bfloat16 [32, 1024, 1024], P(('jown', 'pown')), may hold values from -6 to 6
- bare: bfloat16 [32, 1024, 1024], P(('jown', 'pown')), may hold values from -0.1875 to 0.1875
- pp_prop: float32 [32, 1024], P(('jown', 'pown')), may hold values from 0.3 to 3
- ph_prop: float32 [32, 1024], P(('jown', 'pown')), may hold values from 0.3 to 3
- orders: int32 [32], replicated, may hold values from 512 to 1024, as said below
- pandya_src: int32 [32, 4], replicated, may hold values from 0 to 31
- pandya_sixj: float32 [32, 4, 1024], P(None, None, ('jown', 'pown')), may hold values from -1 to 1
- back_src: int32 [32, 4], replicated, may hold values from 0 to 31
- back_sixj: float32 [32, 4, 1024], P(None, None, ('jown', 'pown')), may hold values from -1 to 1
Outputs:
- updated: bfloat16 [32, 1024, 1024], P(('jown', 'pown'))
The draws below stay inside these ranges and needn't reach their ends.
Inputs may be any that keep to these rules, and one draw needn't show every extreme that they name: `orders`: some block has order exactly 1024.
All inputs are finite; a program needn't handle non-finite values.
Results may differ from the reference program's by a relative error of at most 0.0055.
Values may be sent and summed in bfloat16 or wider, within the bound.
No kernel may reach another device: no remote copies, remote signals or barrier semaphores. Data moves between devices by JAX's collectives and lax.ppermute only.
A program may use at most 64 MiB of HBM per device.

```python
import math
import jax
import jax.numpy as jnp
from jax import lax

M = 1024
TERMS = 4
BLOCKS = 32


def draw_orders(key, part):
    first_key, second_key = jax.random.split(jax.random.fold_in(key, 17))
    base = jax.random.randint(first_key, (BLOCKS,), M // 2, M + 1)
    chosen = jax.random.randint(second_key, (), 0, BLOCKS)
    return base.at[chosen].set(M).astype(jnp.int32)


def with_ends(drawn, key, least, largest):
    shape = drawn.shape
    place = [jax.random.randint(jax.random.fold_in(key, axis), (), 0, shape[axis]) for axis in range(len(shape))]
    drawn = drawn.at[tuple(place)].set(least)
    longest = shape.index(max(shape))
    place[longest] = (place[longest] + 1) % shape[longest]
    return drawn.at[tuple(place)].set(largest)


def steps_of(rng, shape, cuts, smallest, high):
    gain, own = 1.0, jax.random.fold_in(rng, 6)
    for position, blocks in cuts:
        steps = jnp.exp(jax.random.uniform(jax.random.fold_in(own, position), (blocks,), jnp.float32, smallest / len(cuts), high / len(cuts)))
        gain = gain * jnp.repeat(steps, shape[position] // blocks).reshape([-1 if axis == position else 1 for axis in range(len(shape))])
    return gain


def bell_draw(own_key, extent, spread, limit, shards=(), dtype=jnp.bfloat16):
    level = steps_of(own_key, extent, shards, -0.22, 0.18) if shards else 1.0
    values = jax.random.normal(own_key, extent, jnp.float32) * spread * level
    return jnp.minimum(jnp.maximum(values, -limit), limit).astype(dtype)


def setup_inputs(seed: int = 0) -> dict:
    streams_of = jax.random.split(jax.random.key(seed), 10)
    return {
        "vertex": bell_draw(streams_of[0], (BLOCKS, M, M), 1.0, 6.0, ((0, 32),)),
        "bare": bell_draw(streams_of[1], (BLOCKS, M, M), M ** -0.5, 0.1875, ((0, 32),)),
        "pp_prop": jnp.clip(jnp.exp(math.log(3.0) - 2.3025851 * jax.random.uniform(streams_of[2], (BLOCKS, M), jnp.float32) ** steps_of(streams_of[2], (BLOCKS, M), ((0, 32),), -0.2, 0.2)), 0.3, 3.0),
        "ph_prop": jnp.clip(jnp.exp(math.log(3.0) - 2.3025851 * jax.random.uniform(streams_of[3], (BLOCKS, M), jnp.float32) ** steps_of(streams_of[3], (BLOCKS, M), ((0, 32),), -0.2, 0.2)), 0.3, 3.0),
        "orders": draw_orders(jax.random.fold_in(streams_of[9], 71), 0),
        "pandya_src": with_ends(jax.random.randint(streams_of[5], (BLOCKS, TERMS), 0, BLOCKS), jax.random.fold_in(streams_of[5], 1), 0, BLOCKS - 1).astype(jnp.int32),
        "pandya_sixj": jnp.clip(jax.random.uniform(streams_of[6], (BLOCKS, TERMS, M), jnp.float32, -1.0, 1.0) * steps_of(streams_of[6], (BLOCKS, TERMS, M), ((2, 32),), -0.4, 0.0), -1.0, 1.0),
        "back_src": with_ends(jax.random.randint(streams_of[7], (BLOCKS, TERMS), 0, BLOCKS), jax.random.fold_in(streams_of[7], 1), 0, BLOCKS - 1).astype(jnp.int32),
        "back_sixj": jnp.clip(jax.random.uniform(streams_of[8], (BLOCKS, TERMS, M), jnp.float32, -1.0, 1.0) * steps_of(streams_of[8], (BLOCKS, TERMS, M), ((2, 32),), -0.4, 0.0), -1.0, 1.0),
    }


def pair_mask(order):
    live = (jnp.arange(M) < order).astype(jnp.float32)
    return live[:, None] * live[None, :]

def recouple(blocks, sources, factors, orders):

    def single(item):
        picks, weights, order = item
        summed = jnp.zeros((M, M), jnp.float32)
        for term in range(picks.shape[0]):
            summed = summed + weights[term][:, None] * blocks[picks[term]].astype(jnp.float32)
        return (summed * pair_mask(order)).astype(jnp.bfloat16)
    return lax.map(single, (sources, factors, orders))

def reference(vertex, bare, pp_prop, ph_prop, orders, pandya_src, pandya_sixj, back_src, back_sixj):

    def mask_one(item):
        block, order = item
        return (block.astype(jnp.float32) * pair_mask(order)).astype(jnp.bfloat16)
    masked = lax.map(mask_one, (vertex, orders))
    ph = recouple(masked, pandya_src, pandya_sixj, orders)

    def cycle_one(item):
        block, prop = item
        weighted = (block.astype(jnp.float32) * prop[None, :]).astype(jnp.bfloat16)
        product = jnp.dot(weighted, block, preferred_element_type=jnp.float32)
        return (product * (1.0 / math.sqrt(M))).astype(jnp.bfloat16)
    cycle = lax.map(cycle_one, (ph, ph_prop))
    returned = recouple(cycle, back_src, back_sixj, orders)

    def final_one(item):
        block, interaction, prop, back, order = item
        scaled = (prop[:, None] * block.astype(jnp.float32)).astype(jnp.bfloat16)
        ladder = jnp.dot(interaction, scaled, preferred_element_type=jnp.float32)
        total = block.astype(jnp.float32) + ladder + back.astype(jnp.float32)
        return (total * pair_mask(order)).astype(jnp.bfloat16)
    return lax.map(final_one, (masked, bare, pp_prop, returned, orders))
```

```python
import math

import jax
import jax.numpy as jnp
from jax import lax
from jax.experimental import pallas as pl
from jax.experimental.pallas import tpu as pltpu
from jax.sharding import PartitionSpec as P

AXES = ("jown", "pown")


def recouple_body(src, orders, first, factors, tiles, mixed):
    total, rows, width = tiles.shape
    terms = src.shape[1]
    row_ids = first[0] + lax.broadcasted_iota(jnp.int32, (rows, 1), 0)
    col_ids = lax.broadcasted_iota(jnp.int32, (1, width), 1)

    def one(c, carry):
        own = orders[c]
        weights = factors[c]
        summed = jnp.zeros((rows, width), jnp.float32)
        for k in range(terms):
            pick = src[c, k]
            live = jnp.minimum(own, orders[pick])
            weight = jnp.where(row_ids < live, weights[:, k : k + 1], 0.0)
            part = weight * tiles[pick].astype(jnp.float32)
            summed = summed + jnp.where(col_ids < live, part, 0.0)
        mixed[c] = summed.astype(jnp.bfloat16)
        return carry

    lax.fori_loop(0, total, one, 0)


def recouple_tiles(tiles, src, factors, orders):
    total, rows, width = tiles.shape
    first = (lax.axis_index(AXES) * rows).reshape(1)
    smem = pl.BlockSpec(memory_space=pltpu.SMEM)
    vmem = pl.BlockSpec(memory_space=pltpu.VMEM)
    return pl.pallas_call(
        recouple_body,
        out_shape=jax.ShapeDtypeStruct((total, rows, width), jnp.bfloat16),
        in_specs=[smem, smem, smem, vmem, vmem],
        out_specs=vmem,
        cost_estimate=pl.CostEstimate(
            flops=8 * total * rows * width,
            bytes_accessed=4 * total * rows * width,
            transcendentals=0,
        ),
    )(src, orders, first, jnp.swapaxes(factors, 1, 2), tiles)


def ladder_body(order, bare, vertex, prop, base, scaled):
    rows, width = base.shape
    step = pl.program_id(0)
    own = order[0]
    row_ids = lax.broadcasted_iota(jnp.int32, (width, 1), 0)
    col_ids = lax.broadcasted_iota(jnp.int32, (1, width), 1)

    @pl.when(step == 0)
    def _():
        def fill(i, carry):
            at = pl.ds(pl.multiple_of(i * rows, rows), rows)
            ids = i * rows + lax.broadcasted_iota(jnp.int32, (rows, 1), 0)
            weight = jnp.where(ids < own, prop[at, :], 0.0)
            part = weight * vertex[at, :].astype(jnp.float32)
            scaled[at, :] = jnp.where(col_ids < own, part, 0.0).astype(jnp.bfloat16)
            return carry

        lax.fori_loop(0, width // rows, fill, 0)

    at = pl.ds(pl.multiple_of(step * rows, rows), rows)
    product = jnp.dot(bare[...], scaled[...], preferred_element_type=jnp.float32)
    total = vertex[at, :].astype(jnp.float32) + product
    live = (step * rows + row_ids[:rows] < own) & (col_ids < own)
    base[...] = jnp.where(live, total, 0.0)


def ladder_base(order, bare, vertex, prop):
    width = vertex.shape[0]
    rows = min(256, width)
    whole = pl.BlockSpec((width, width), lambda i: (0, 0))
    return pl.pallas_call(
        ladder_body,
        grid=(width // rows,),
        out_shape=jax.ShapeDtypeStruct((width, width), jnp.float32),
        in_specs=[
            pl.BlockSpec(memory_space=pltpu.SMEM),
            pl.BlockSpec((rows, width), lambda i: (i, 0)),
            whole,
            pl.BlockSpec((width, 1), lambda i: (0, 0)),
        ],
        out_specs=pl.BlockSpec((rows, width), lambda i: (i, 0)),
        scratch_shapes=[pltpu.VMEM((width, width), jnp.bfloat16)],
        cost_estimate=pl.CostEstimate(
            flops=2 * width**3, bytes_accessed=8 * width * width, transcendentals=0
        ),
    )(order, bare, vertex, prop)


def exchange(tiles):
    return lax.all_to_all(tiles, AXES, split_axis=0, concat_axis=0, tiled=True)


def per_device(
    vertex, bare, pp_prop, ph_prop, orders, pandya_src, pandya_sixj, back_src, back_sixj
):
    per_owner, width, _ = vertex.shape
    parts = lax.axis_size(AXES)
    tile_rows = width // parts
    assert per_owner == 1
    own_order = lax.dynamic_slice_in_dim(orders, lax.axis_index(AXES), 1)

    def to_tiles(block):
        return block.reshape(parts, tile_rows, width)

    def to_block(tiles):
        return tiles.reshape(width, width)

    tiles = exchange(to_tiles(vertex[0]))
    ph = to_block(exchange(recouple_tiles(tiles, pandya_src, pandya_sixj, orders)))
    weighted = (ph.astype(jnp.float32) * ph_prop).astype(jnp.bfloat16)
    product = jnp.dot(weighted, ph, preferred_element_type=jnp.float32)
    cycle = (product * (1.0 / math.sqrt(width))).astype(jnp.bfloat16)
    tiles = exchange(to_tiles(cycle))
    returned = to_block(exchange(recouple_tiles(tiles, back_src, back_sixj, orders)))
    base = ladder_base(own_order, bare[0], vertex[0], pp_prop.reshape(width, 1))
    return (base + returned.astype(jnp.float32)).astype(jnp.bfloat16)[None]


def solution(mesh):
    placed = (
        P(AXES, None, None),
        P(AXES, None, None),
        P(AXES, None),
        P(AXES, None),
        P(),
        P(),
        P(None, None, AXES),
        P(),
        P(None, None, AXES),
    )
    return jax.shard_map(
        per_device,
        mesh=mesh,
        in_specs=placed,
        out_specs=P(AXES, None, None),
        check_vma=False,
    )
```

```python
import functools
import math

import jax
import jax.numpy as jnp
from jax import lax
from jax.experimental import pallas as pl
from jax.experimental.pallas import tpu as pltpu
from jax.sharding import PartitionSpec as P

AXES = ("jown", "pown")
LEAST_ORDER = 512


GRANT = 20 * 2**20


def in_hbm(x):
    return pltpu.with_memory_space_constraint(x, pltpu.HBM)


def recouple_body(masked, src, orders, first, factors, tiles, mixed):
    group, rows, width = mixed.shape
    terms = src.shape[1]
    lanes = min(256, width)
    base = pl.program_id(0) * group
    row_ids = first[0] + lax.broadcasted_iota(jnp.int32, (rows, 1), 0)

    def one(at_c, carry):
        c = base + at_c
        own = orders[c]
        weights = factors[c]
        picks, lives, scales = [], [], []
        for k in range(terms):
            pick = src[c, k]
            live = own if masked else jnp.minimum(own, orders[pick])
            weight = jnp.where(row_ids < live, weights[:, k : k + 1], 0.0)
            picks.append(pick)
            lives.append(live)
            scales.append(jnp.broadcast_to(weight, (rows, lanes)))
        for start in range(0, width, lanes):
            at = pl.ds(start, lanes)
            edge = start + lanes > LEAST_ORDER
            ids = start + lax.broadcasted_iota(jnp.int32, (1, lanes), 1)
            summed = None
            for k in range(terms):
                part = scales[k] * tiles[picks[k], :, at].astype(jnp.float32)
                if edge and not masked:
                    part = jnp.where(ids < lives[k], part, 0.0)
                summed = part if summed is None else summed + part
            if edge and masked:
                summed = jnp.where(ids < own, summed, 0.0)
            mixed[at_c, :, at] = summed.astype(jnp.bfloat16)
        return carry

    lax.fori_loop(0, group, one, 0, unroll=4)


def recouple_tiles(tiles, src, factors, orders, masked):
    total, rows, width = tiles.shape
    group = max(g for g in range(1, total // 4 + 1) if total % g == 0)
    first = (lax.axis_index(AXES) * rows).reshape(1)
    smem = pl.BlockSpec(memory_space=pltpu.SMEM)
    vmem = pl.BlockSpec(memory_space=pltpu.VMEM)
    return pl.pallas_call(
        functools.partial(recouple_body, masked),
        grid=(total // group,),
        out_shape=pltpu.HBM((total, rows, width), jnp.bfloat16),
        in_specs=[smem, smem, smem, vmem, vmem],
        out_specs=pl.BlockSpec((group, rows, width), lambda i: (i, 0, 0)),
        compiler_params=pltpu.CompilerParams(vmem_limit_bytes=GRANT),
        cost_estimate=pl.CostEstimate(
            flops=8 * total * rows * width,
            bytes_accessed=4 * total * rows * width,
            transcendentals=0,
        ),
    )(src, orders, first, jnp.swapaxes(factors, 1, 2), tiles)


def cycle_body(prop, ph, cycle):
    rows, width = cycle.shape
    at = pl.ds(pl.multiple_of(pl.program_id(0) * rows, rows), rows)
    weighted = (ph[at, :].astype(jnp.float32) * prop[...]).astype(jnp.bfloat16)
    product = jnp.dot(weighted, ph[...], preferred_element_type=jnp.float32)
    cycle[...] = (product * (1.0 / math.sqrt(width))).astype(jnp.bfloat16)


def cycle_block(prop, ph):
    width = ph.shape[1]
    rows = min(256, width)
    vmem = pl.BlockSpec(memory_space=pltpu.VMEM)
    return pl.pallas_call(
        cycle_body,
        grid=(width // rows,),
        out_shape=pltpu.HBM(ph.shape, jnp.bfloat16),
        in_specs=[vmem, vmem],
        out_specs=pl.BlockSpec((rows, width), lambda i: (i, 0)),
        compiler_params=pltpu.CompilerParams(vmem_limit_bytes=GRANT),
        cost_estimate=pl.CostEstimate(
            flops=2 * ph.size * width, bytes_accessed=4 * ph.size, transcendentals=0
        ),
    )(prop, ph)


def finish_body(base, returned, updated):
    total = base[...] + returned[...].astype(jnp.float32)
    updated[...] = total.astype(jnp.bfloat16)


def finish(base, returned):
    width = base.shape[1]
    rows = min(512, width)
    block = pl.BlockSpec((rows, width), lambda i: (i, 0))
    return pl.pallas_call(
        finish_body,
        grid=(width // rows,),
        out_shape=pltpu.HBM(base.shape, jnp.bfloat16),
        in_specs=[block, block],
        out_specs=block,
        compiler_params=pltpu.CompilerParams(vmem_limit_bytes=GRANT),
        cost_estimate=pl.CostEstimate(
            flops=2 * base.size, bytes_accessed=8 * base.size, transcendentals=0
        ),
    )(in_hbm(base), in_hbm(returned))


def ladder_body(order, bare, vertex, prop, base, scaled):
    rows, width = bare.shape
    step = pl.program_id(0)
    own = order[0]
    row_ids = lax.broadcasted_iota(jnp.int32, (width, 1), 0)
    col_ids = lax.broadcasted_iota(jnp.int32, (1, width), 1)

    @pl.when(step == 0)
    def _():
        def fill(i, carry):
            at = pl.ds(pl.multiple_of(i * rows, rows), rows)
            ids = i * rows + lax.broadcasted_iota(jnp.int32, (rows, 1), 0)
            weight = jnp.where(ids < own, prop[at, :], 0.0)
            part = weight * vertex[at, :].astype(jnp.float32)
            scaled[at, :] = jnp.where(col_ids < own, part, 0.0).astype(jnp.bfloat16)
            return carry

        lax.fori_loop(0, width // rows, fill, 0)

    at = pl.ds(pl.multiple_of(step * rows, rows), rows)
    product = jnp.dot(bare[...], scaled[...], preferred_element_type=jnp.float32)
    total = vertex[at, :].astype(jnp.float32) + product
    live = (step * rows + row_ids[:rows] < own) & (col_ids < own)
    base[...] = jnp.where(live, total, 0.0)


def ladder_base(order, bare, vertex, prop):
    width = vertex.shape[0]
    rows = min(256, width)
    whole = pl.BlockSpec((width, width), lambda i: (0, 0))
    return pl.pallas_call(
        ladder_body,
        grid=(width // rows,),
        out_shape=pltpu.HBM((width, width), jnp.float32),
        in_specs=[
            pl.BlockSpec(memory_space=pltpu.SMEM),
            pl.BlockSpec((rows, width), lambda i: (i, 0)),
            whole,
            pl.BlockSpec((width, 1), lambda i: (0, 0)),
        ],
        out_specs=pl.BlockSpec((rows, width), lambda i: (i, 0)),
        scratch_shapes=[pltpu.VMEM((width, width), jnp.bfloat16)],
        compiler_params=pltpu.CompilerParams(vmem_limit_bytes=GRANT),
        cost_estimate=pl.CostEstimate(
            flops=2 * width**3, bytes_accessed=8 * width * width, transcendentals=0
        ),
    )(order, bare, vertex, prop)


def exchange(tiles):
    return lax.all_to_all(tiles, AXES, split_axis=0, concat_axis=0, tiled=True)


def per_device(
    vertex, bare, pp_prop, ph_prop, orders, pandya_src, pandya_sixj, back_src, back_sixj
):
    per_owner, width, _ = vertex.shape
    parts = lax.axis_size(AXES)
    tile_rows = width // parts
    assert per_owner == 1
    own_order = lax.dynamic_slice_in_dim(orders, lax.axis_index(AXES), 1)

    def to_tiles(block):
        return block.reshape(parts, tile_rows, width)

    def to_block(tiles):
        return tiles.reshape(width, width)

    tiles = exchange(to_tiles(vertex[0]))
    ph = to_block(exchange(recouple_tiles(tiles, pandya_src, pandya_sixj, orders, False)))
    cycle = cycle_block(ph_prop, ph)
    tiles = exchange(to_tiles(cycle))
    returned = to_block(exchange(recouple_tiles(tiles, back_src, back_sixj, orders, True)))
    base = ladder_base(own_order, bare[0], vertex[0], pp_prop.reshape(width, 1))
    return finish(base, returned)[None]


def solution(mesh):
    placed = (
        P(AXES, None, None),
        P(AXES, None, None),
        P(AXES, None),
        P(AXES, None),
        P(),
        P(),
        P(None, None, AXES),
        P(),
        P(None, None, AXES),
    )
    return jax.shard_map(
        per_device,
        mesh=mesh,
        in_specs=placed,
        out_specs=P(AXES, None, None),
        check_vma=False,
    )
```

```python
import functools
import math

import jax
import jax.numpy as jnp
from jax import lax
from jax.experimental import pallas as pl
from jax.experimental.pallas import tpu as pltpu
from jax.sharding import PartitionSpec as P


AXES = ("jown", "pown")
LEAST_ORDER = 512


GRANT = 20 * 2**20
SHARE = 4


def in_hbm(x):
    return pltpu.with_memory_space_constraint(x, pltpu.HBM)


def digits():
    low = lax.axis_size("pown").bit_length() - 1
    high = lax.axis_size("jown").bit_length() - 1
    assert 1 << low == lax.axis_size("pown") and 1 << high == lax.axis_size("jown")
    first = list(range(low))[-2:]
    last = [low] if high else []
    middle = [b for b in range(low + high) if b not in first + last]
    return [group for group in (first, middle, last) if group]


def place(tile, me, groups):
    relative = tile ^ me
    at = relative * 0
    for group in groups:
        for bit in reversed(group):
            at = at * 2 + ((relative >> bit) & 1)
    return at


def small_exchange(tiles, groups):
    total = tiles.shape[0]
    sizes = [1 << len(group) for group in groups]
    tiles = tiles.reshape(*sizes, *tiles.shape[1:])
    for axis, group in enumerate(groups):
        got = [lax.index_in_dim(tiles, 0, axis, keepdims=False)]
        for digit in range(1, sizes[axis]):
            mask = sum(((digit >> i) & 1) << bit for i, bit in enumerate(group))
            sent = lax.index_in_dim(tiles, digit, axis, keepdims=False)
            pairs = [(d, d ^ mask) for d in range(total)]
            got.append(lax.ppermute(sent, AXES, pairs))
        tiles = jnp.stack(got, axis)
    return tiles.reshape(total, *tiles.shape[len(sizes) :])


def small_columns(width):
    return max(128, width // SHARE // 128 * 128)


def pack_body(groups, me, block, small, large):
    columns = small.shape[2]
    group = block.shape[0]

    def one(t, carry):
        to = place(pl.program_id(0) * group + t, me[0], groups)
        small[to] = block[t, :, :columns]
        large[t] = block[t, :, columns:]
        return carry

    lax.fori_loop(0, group, one, 0, unroll=4)


def pack(me, tiles, groups):
    total, rows, width = tiles.shape
    columns = small_columns(width)
    group = total // 4 if total % 4 == 0 else total
    return pl.pallas_call(
        functools.partial(pack_body, groups),
        grid=(total // group,),
        out_shape=(
            pltpu.HBM((total, rows, columns), tiles.dtype),
            pltpu.HBM((total, rows, width - columns), tiles.dtype),
        ),
        in_specs=[
            pl.BlockSpec(memory_space=pltpu.SMEM),
            pl.BlockSpec((group, rows, width), lambda i: (i, 0, 0)),
        ],
        out_specs=(
            pl.BlockSpec((total, rows, columns), lambda i: (0, 0, 0)),
            pl.BlockSpec((group, rows, width - columns), lambda i: (i, 0, 0)),
        ),
        compiler_params=pltpu.CompilerParams(vmem_limit_bytes=GRANT),
        cost_estimate=pl.CostEstimate(
            flops=0, bytes_accessed=4 * total * rows * width, transcendentals=0
        ),
    )(me, tiles)


def recouple_body(masked, groups, left, src, orders, me, factors, tiles, mixed):
    group, rows, width = mixed.shape
    terms = src.shape[1]
    lanes = 256 if width % 256 == 0 else 128
    base = pl.program_id(0) * group
    row_ids = me[0] * rows + lax.broadcasted_iota(jnp.int32, (rows, 1), 0)

    def one(at_c, carry):
        c = base + at_c
        own = orders[c]
        weights = factors[c]
        picks, lives, scales = [], [], []
        for k in range(terms):
            pick = src[c, k]
            live = own if masked else jnp.minimum(own, orders[pick])
            weight = jnp.where(row_ids < live, weights[:, k : k + 1], 0.0)
            picks.append(place(pick, me[0], groups) if groups else pick)
            lives.append(live)
            scales.append(jnp.broadcast_to(weight, (rows, lanes)))
        to = place(c, me[0], groups) if groups else at_c
        for start in range(0, width, lanes):
            at = pl.ds(start, lanes)
            edge = left + start + lanes > LEAST_ORDER
            ids = left + start + lax.broadcasted_iota(jnp.int32, (1, lanes), 1)
            summed = None
            for k in range(terms):
                part = scales[k] * tiles[picks[k], :, at].astype(jnp.float32)
                if edge and not masked:
                    part = jnp.where(ids < lives[k], part, 0.0)
                summed = part if summed is None else summed + part
            if edge and masked:
                summed = jnp.where(ids < own, summed, 0.0)
            mixed[to, :, at] = summed.astype(jnp.bfloat16)
        return carry

    lax.fori_loop(0, group, one, 0, unroll=4)


def recouple_tiles(me, tiles, src, factors, orders, masked, groups, left):
    total, rows, width = tiles.shape
    if groups:
        group = total
    else:
        group = max(g for g in range(1, total // 4 + 1) if total % g == 0)
    smem = pl.BlockSpec(memory_space=pltpu.SMEM)
    vmem = pl.BlockSpec(memory_space=pltpu.VMEM)
    return pl.pallas_call(
        functools.partial(recouple_body, masked, groups, left),
        grid=(total // group,),
        out_shape=pltpu.HBM((total, rows, width), jnp.bfloat16),
        in_specs=[smem, smem, smem, vmem, vmem],
        out_specs=pl.BlockSpec((group, rows, width), lambda i: (i, 0, 0)),
        compiler_params=pltpu.CompilerParams(vmem_limit_bytes=GRANT),
        cost_estimate=pl.CostEstimate(
            flops=8 * total * rows * width,
            bytes_accessed=4 * total * rows * width,
            transcendentals=0,
        ),
    )(src, orders, me, factors, tiles)


def cycle_body(groups, me, prop, small, large, small_out, large_out, ph):
    step = pl.program_id(0)
    total, rows, columns = small.shape
    width = ph.shape[1]
    group = large_out.shape[0]

    @pl.when(step == 0)
    def _():
        def one(t, carry):
            at = pl.ds(pl.multiple_of(t * rows, rows), rows)
            ph[at, :columns] = small[place(t, me[0], groups)]
            ph[at, columns:] = large[t]
            return carry

        lax.fori_loop(0, total, one, 0, unroll=4)

    height = group * rows
    at = pl.ds(pl.multiple_of(step * height, height), height)
    weighted = (ph[at, :].astype(jnp.float32) * prop[...]).astype(jnp.bfloat16)
    product = jnp.dot(weighted, ph[...], preferred_element_type=jnp.float32)
    cycle = (product * (1.0 / math.sqrt(width))).astype(jnp.bfloat16)
    large_out[...] = cycle[:, columns:].reshape(large_out.shape)
    for t in range(group):
        to = place(step * group + t, me[0], groups)
        small_out[to] = cycle[t * rows : (t + 1) * rows, :columns]


def cycle_block(me, prop, small, large, groups):
    total, rows, columns = small.shape
    width = total * rows
    group = max(g for g in range(1, total // 4 + 1) if total % g == 0)
    vmem = pl.BlockSpec(memory_space=pltpu.VMEM)
    return pl.pallas_call(
        functools.partial(cycle_body, groups),
        grid=(total // group,),
        out_shape=(
            pltpu.HBM(small.shape, jnp.bfloat16),
            pltpu.HBM(large.shape, jnp.bfloat16),
        ),
        in_specs=[pl.BlockSpec(memory_space=pltpu.SMEM), vmem, vmem, vmem],
        out_specs=(
            pl.BlockSpec(small.shape, lambda i: (0, 0, 0)),
            pl.BlockSpec((group, rows, width - columns), lambda i: (i, 0, 0)),
        ),
        scratch_shapes=[pltpu.VMEM((width, width), jnp.bfloat16)],
        compiler_params=pltpu.CompilerParams(vmem_limit_bytes=GRANT),
        cost_estimate=pl.CostEstimate(
            flops=2 * width**3, bytes_accessed=4 * width * width, transcendentals=0
        ),
    )(me, prop, small, large)


def finish_body(groups, me, base, small, large, updated):
    step = pl.program_id(0)
    group, rows, _ = large.shape
    columns = small.shape[2]

    def one(t, carry):
        at = pl.ds(pl.multiple_of(t * rows, rows), rows)
        part = small[place(step * group + t, me[0], groups)].astype(jnp.float32)
        updated[at, :columns] = (base[at, :columns] + part).astype(jnp.bfloat16)
        part = large[t].astype(jnp.float32)
        updated[at, columns:] = (base[at, columns:] + part).astype(jnp.bfloat16)
        return carry

    lax.fori_loop(0, group, one, 0, unroll=4)


def finish(me, base, small, large, groups):
    total, rows, columns = small.shape
    width = base.shape[1]
    group = total // 2
    block = pl.BlockSpec((group * rows, width), lambda i: (i, 0))
    return pl.pallas_call(
        functools.partial(finish_body, groups),
        grid=(total // group,),
        out_shape=pltpu.HBM(base.shape, jnp.bfloat16),
        in_specs=[
            pl.BlockSpec(memory_space=pltpu.SMEM),
            block,
            pl.BlockSpec(memory_space=pltpu.VMEM),
            pl.BlockSpec((group, rows, width - columns), lambda i: (i, 0, 0)),
        ],
        out_specs=block,
        compiler_params=pltpu.CompilerParams(vmem_limit_bytes=GRANT),
        cost_estimate=pl.CostEstimate(
            flops=2 * base.size, bytes_accessed=8 * base.size, transcendentals=0
        ),
    )(me, in_hbm(base), small, in_hbm(large))


def ladder_body(order, bare, vertex, prop, base, scaled):
    rows, width = bare.shape
    step = pl.program_id(0)
    own = order[0]
    row_ids = lax.broadcasted_iota(jnp.int32, (width, 1), 0)
    col_ids = lax.broadcasted_iota(jnp.int32, (1, width), 1)

    @pl.when(step == 0)
    def _():
        def fill(i, carry):
            at = pl.ds(pl.multiple_of(i * rows, rows), rows)
            ids = i * rows + lax.broadcasted_iota(jnp.int32, (rows, 1), 0)
            weight = jnp.where(ids < own, prop[at, :], 0.0)
            part = weight * vertex[at, :].astype(jnp.float32)
            scaled[at, :] = jnp.where(col_ids < own, part, 0.0).astype(jnp.bfloat16)
            return carry

        lax.fori_loop(0, width // rows, fill, 0)

    at = pl.ds(pl.multiple_of(step * rows, rows), rows)
    product = jnp.dot(bare[...], scaled[...], preferred_element_type=jnp.float32)
    total = vertex[at, :].astype(jnp.float32) + product
    live = (step * rows + row_ids[:rows] < own) & (col_ids < own)
    base[...] = jnp.where(live, total, 0.0)


def ladder_base(order, bare, vertex, prop):
    width = vertex.shape[0]
    rows = min(256, width)
    whole = pl.BlockSpec((width, width), lambda i: (0, 0))
    return pl.pallas_call(
        ladder_body,
        grid=(width // rows,),
        out_shape=pltpu.HBM((width, width), jnp.float32),
        in_specs=[
            pl.BlockSpec(memory_space=pltpu.SMEM),
            pl.BlockSpec((rows, width), lambda i: (i, 0)),
            whole,
            pl.BlockSpec((width, 1), lambda i: (0, 0)),
        ],
        out_specs=pl.BlockSpec((rows, width), lambda i: (i, 0)),
        scratch_shapes=[pltpu.VMEM((width, width), jnp.bfloat16)],
        compiler_params=pltpu.CompilerParams(vmem_limit_bytes=GRANT),
        cost_estimate=pl.CostEstimate(
            flops=2 * width**3, bytes_accessed=8 * width * width, transcendentals=0
        ),
    )(order, bare, vertex, prop)


def exchange(tiles):
    return lax.all_to_all(tiles, AXES, split_axis=0, concat_axis=0, tiled=True)


def per_device(
    vertex, bare, pp_prop, ph_prop, orders, pandya_src, pandya_sixj, back_src, back_sixj
):
    per_owner, width, _ = vertex.shape
    parts = lax.axis_size(AXES)
    rows = width // parts
    assert per_owner == 1
    groups = digits()
    me = lax.axis_index(AXES).reshape(1)
    columns = small_columns(width)
    own_order = lax.dynamic_slice_in_dim(orders, me[0], 1)

    def recouple(small, large, src, sixj, masked):
        factors = jnp.swapaxes(sixj, 1, 2)
        small = small_exchange(small, groups)
        large = exchange(large)
        small = recouple_tiles(me, small, src, factors, orders, masked, groups, 0)
        small = small_exchange(small, groups)
        large = recouple_tiles(me, large, src, factors, orders, masked, None, columns)
        large = exchange(large)
        return small, large

    tiles = vertex[0].reshape(parts, rows, width)
    small, large = pack(me, tiles, groups)
    small, large = recouple(small, large, pandya_src, pandya_sixj, False)
    small, large = cycle_block(me, ph_prop, small, large, groups)
    small, large = recouple(small, large, back_src, back_sixj, True)
    prop = pp_prop.reshape(width, 1)
    base = ladder_base(own_order, bare[0], vertex[0], prop)
    return finish(me, base, small, large, groups)[None]


def solution(mesh):
    placed = (
        P(AXES, None, None),
        P(AXES, None, None),
        P(AXES, None),
        P(AXES, None),
        P(),
        P(),
        P(None, None, AXES),
        P(),
        P(None, None, AXES),
    )
    return jax.shard_map(
        per_device,
        mesh=mesh,
        in_specs=placed,
        out_specs=P(AXES, None, None),
        check_vma=False,
    )
```

```python
import functools
import math

import jax
import jax.numpy as jnp
from jax import lax
from jax.experimental import pallas as pl
from jax.experimental.pallas import tpu as pltpu
from jax.sharding import PartitionSpec as P


AXES = ("jown", "pown")
LEAST_ORDER = 512


GRANT = 20 * 2**20
SHARE = 4


def in_hbm(x):
    return pltpu.with_memory_space_constraint(x, pltpu.HBM)


def digits():
    low = lax.axis_size("pown").bit_length() - 1
    high = lax.axis_size("jown").bit_length() - 1
    assert 1 << low == lax.axis_size("pown") and 1 << high == lax.axis_size("jown")
    first = list(range(low))[-2:]
    last = [low] if high else []
    middle = [b for b in range(low + high) if b not in first + last]
    return [group for group in (first, middle, last) if group]


def place(tile, me, groups):
    relative = tile ^ me
    at = relative * 0
    for group in groups:
        for bit in reversed(group):
            at = at * 2 + ((relative >> bit) & 1)
    return at


def unplace(at, groups):
    relative = at * 0
    for group in reversed(groups):
        for bit in group:
            relative = relative | ((at & 1) << bit)
            at = at >> 1
    return relative


def mask_of(digit, group):
    return sum(((digit >> i) & 1) << bit for i, bit in enumerate(group))


def small_exchange(pieces, groups):
    total = len(pieces) * pieces[0].shape[0]
    sizes = [1 << len(group) for group in groups]
    tail = pieces[0].shape[1:]
    tiles = None
    for axis, group in enumerate(groups):
        got = []
        for digit in range(sizes[axis]):
            if axis:
                sent = lax.index_in_dim(tiles, digit, axis, keepdims=False)
            else:
                sent = pieces[digit].reshape(*sizes[1:], *tail)
            if digit:
                mask = mask_of(digit, group)
                pairs = [(d, d ^ mask) for d in range(total)]
                sent = lax.ppermute(sent, AXES, pairs)
            got.append(sent)
        tiles = jnp.stack(got, axis)
    return tiles.reshape(total, *tail)


def small_columns(width):
    return max(128, width // SHARE // 128 * 128)


def scatter(me, groups, pieces, write):
    for digit, piece in enumerate(pieces):
        first = mask_of(digit, groups[0])

        def one(q, carry, piece=piece, first=first):
            write(piece, q, (unplace(q, groups[1:]) | first) ^ me)
            return carry

        lax.fori_loop(0, piece.shape[0], one, 0, unroll=4)


def pieces_of(total, groups, tail):
    digits_of = 1 << len(groups[0])
    shape = (total // digits_of, *tail)
    block = pl.BlockSpec(shape, lambda i: (0,) * len(shape))
    return (pltpu.HBM(shape, jnp.bfloat16),) * digits_of, (block,) * digits_of


def pack_body(groups, me, block, *pieces):
    def write(piece, q, tile):
        piece[q] = block[tile]

    scatter(me[0], groups, pieces, write)


def pack_small(me, tiles, groups):
    total, rows, width = tiles.shape
    columns = small_columns(width)
    shapes, specs = pieces_of(total, groups, (rows, columns))
    return pl.pallas_call(
        functools.partial(pack_body, groups),
        grid=(1,),
        out_shape=shapes,
        in_specs=[
            pl.BlockSpec(memory_space=pltpu.SMEM),
            pl.BlockSpec((total, rows, columns), lambda i: (0, 0, 0)),
        ],
        out_specs=specs,
        compiler_params=pltpu.CompilerParams(vmem_limit_bytes=GRANT),
        cost_estimate=pl.CostEstimate(
            flops=0, bytes_accessed=4 * total * rows * columns, transcendentals=0
        ),
    )(me, in_hbm(tiles))


def pack_large_body(block, large):
    large[...] = block[:, :, block.shape[2] - large.shape[2] :]


def pack_large(tiles):
    total, rows, width = tiles.shape
    group = total // 2
    rest = width - small_columns(width)
    return pl.pallas_call(
        pack_large_body,
        grid=(total // group,),
        out_shape=pltpu.HBM((total, rows, rest), tiles.dtype),
        in_specs=[pl.BlockSpec((group, rows, width), lambda i: (i, 0, 0))],
        out_specs=pl.BlockSpec((group, rows, rest), lambda i: (i, 0, 0)),
        compiler_params=pltpu.CompilerParams(vmem_limit_bytes=GRANT),
        cost_estimate=pl.CostEstimate(
            flops=0, bytes_accessed=4 * total * rows * width, transcendentals=0
        ),
    )(in_hbm(tiles))


def recouple_body(masked, groups, left, src, orders, me, factors, tiles, *mixed):
    width = tiles.shape[2]
    rows = tiles.shape[1]
    terms = src.shape[1]
    lanes = 256 if width % 256 == 0 else 128
    row_ids = me[0] * rows + lax.broadcasted_iota(jnp.int32, (rows, 1), 0)

    def write(out, to, c):
        own = orders[c]
        weights = factors[c]
        picks, lives, scales = [], [], []
        for k in range(terms):
            pick = src[c, k]
            live = own if masked else jnp.minimum(own, orders[pick])
            weight = jnp.where(row_ids < live, weights[:, k : k + 1], 0.0)
            picks.append(place(pick, me[0], groups) if groups else pick)
            lives.append(live)
            scales.append(jnp.broadcast_to(weight, (rows, lanes)))
        for start in range(0, width, lanes):
            at = pl.ds(start, lanes)
            edge = left + start + lanes > LEAST_ORDER
            ids = left + start + lax.broadcasted_iota(jnp.int32, (1, lanes), 1)
            summed = None
            for k in range(terms):
                part = scales[k] * tiles[picks[k], :, at].astype(jnp.float32)
                if edge and not masked:
                    part = jnp.where(ids < lives[k], part, 0.0)
                summed = part if summed is None else summed + part
            if edge and masked:
                summed = jnp.where(ids < own, summed, 0.0)
            out[to, :, at] = summed.astype(jnp.bfloat16)

    if groups:
        scatter(me[0], groups, mixed, write)
        return
    group = mixed[0].shape[0]
    base = pl.program_id(0) * group

    def one(c, carry):
        write(mixed[0], c, base + c)
        return carry

    lax.fori_loop(0, group, one, 0, unroll=4)


def recouple_tiles(me, tiles, src, factors, orders, masked, groups, left):
    total, rows, width = tiles.shape
    if groups:
        group = total
        shapes, specs = pieces_of(total, groups, (rows, width))
    else:
        group = max(g for g in range(1, total // 4 + 1) if total % g == 0)
        shapes = pltpu.HBM((total, rows, width), jnp.bfloat16)
        specs = pl.BlockSpec((group, rows, width), lambda i: (i, 0, 0))
    smem = pl.BlockSpec(memory_space=pltpu.SMEM)
    vmem = pl.BlockSpec(memory_space=pltpu.VMEM)
    return pl.pallas_call(
        functools.partial(recouple_body, masked, groups, left),
        grid=(total // group,),
        out_shape=shapes,
        in_specs=[smem, smem, smem, vmem, vmem],
        out_specs=specs,
        compiler_params=pltpu.CompilerParams(vmem_limit_bytes=GRANT),
        cost_estimate=pl.CostEstimate(
            flops=8 * total * rows * width,
            bytes_accessed=4 * total * rows * width,
            transcendentals=0,
        ),
    )(src, orders, me, factors, tiles)


def cycle_body(groups, me, prop, small, large, large_out, *rest):
    pieces, (ph, kept) = rest[:-2], rest[-2:]
    step = pl.program_id(0)
    total, rows, columns = small.shape
    width = ph.shape[1]
    group = large_out.shape[0]

    @pl.when(step == 0)
    def _():
        def one(t, carry):
            at = pl.ds(pl.multiple_of(t * rows, rows), rows)
            ph[at, :columns] = small[place(t, me[0], groups)]
            ph[at, columns:] = large[t]
            return carry

        lax.fori_loop(0, total, one, 0, unroll=4)

    height = group * rows
    at = pl.ds(pl.multiple_of(step * height, height), height)
    weighted = (ph[at, :].astype(jnp.float32) * prop[...]).astype(jnp.bfloat16)
    product = jnp.dot(weighted, ph[...], preferred_element_type=jnp.float32)
    cycle = (product * (1.0 / math.sqrt(width))).astype(jnp.bfloat16)
    large_out[...] = cycle[:, columns:].reshape(large_out.shape)
    for t in range(group):
        kept[step * group + t] = cycle[t * rows : (t + 1) * rows, :columns]

    @pl.when(step == pl.num_programs(0) - 1)
    def _():
        def write(piece, q, tile):
            piece[q] = kept[tile]

        scatter(me[0], groups, pieces, write)


def cycle_block(me, prop, small, large, groups):
    total, rows, columns = small.shape
    width = total * rows
    group = max(g for g in range(1, total // 4 + 1) if total % g == 0)
    vmem = pl.BlockSpec(memory_space=pltpu.VMEM)
    shapes, specs = pieces_of(total, groups, (rows, columns))
    large_out, *pieces = pl.pallas_call(
        functools.partial(cycle_body, groups),
        grid=(total // group,),
        out_shape=(pltpu.HBM(large.shape, jnp.bfloat16), *shapes),
        in_specs=[pl.BlockSpec(memory_space=pltpu.SMEM), vmem, vmem, vmem],
        out_specs=(
            pl.BlockSpec((group, rows, width - columns), lambda i: (i, 0, 0)),
            *specs,
        ),
        scratch_shapes=[
            pltpu.VMEM((width, width), jnp.bfloat16),
            pltpu.VMEM(small.shape, jnp.bfloat16),
        ],
        compiler_params=pltpu.CompilerParams(vmem_limit_bytes=GRANT),
        cost_estimate=pl.CostEstimate(
            flops=2 * width**3, bytes_accessed=4 * width * width, transcendentals=0
        ),
    )(me, prop, small, large)
    return pieces, large_out


def finish_body(groups, me, base, small, large, updated):
    step = pl.program_id(0)
    group, rows, _ = large.shape
    columns = small.shape[2]

    def one(t, carry):
        at = pl.ds(pl.multiple_of(t * rows, rows), rows)
        part = small[place(step * group + t, me[0], groups)].astype(jnp.float32)
        updated[at, :columns] = (base[at, :columns] + part).astype(jnp.bfloat16)
        part = large[t].astype(jnp.float32)
        updated[at, columns:] = (base[at, columns:] + part).astype(jnp.bfloat16)
        return carry

    lax.fori_loop(0, group, one, 0, unroll=4)


def finish(me, base, small, large, groups):
    total, rows, columns = small.shape
    width = base.shape[1]
    group = total // 2
    block = pl.BlockSpec((group * rows, width), lambda i: (i, 0))
    return pl.pallas_call(
        functools.partial(finish_body, groups),
        grid=(total // group,),
        out_shape=pltpu.HBM(base.shape, jnp.bfloat16),
        in_specs=[
            pl.BlockSpec(memory_space=pltpu.SMEM),
            block,
            pl.BlockSpec(memory_space=pltpu.VMEM),
            pl.BlockSpec((group, rows, width - columns), lambda i: (i, 0, 0)),
        ],
        out_specs=block,
        compiler_params=pltpu.CompilerParams(vmem_limit_bytes=GRANT),
        cost_estimate=pl.CostEstimate(
            flops=2 * base.size, bytes_accessed=8 * base.size, transcendentals=0
        ),
    )(me, in_hbm(base), small, in_hbm(large))


def ladder_body(order, bare, vertex, prop, base, scaled):
    rows, width = bare.shape
    step = pl.program_id(0)
    own = order[0]
    row_ids = lax.broadcasted_iota(jnp.int32, (width, 1), 0)
    col_ids = lax.broadcasted_iota(jnp.int32, (1, width), 1)

    @pl.when(step == 0)
    def _():
        def fill(i, carry):
            at = pl.ds(pl.multiple_of(i * rows, rows), rows)
            ids = i * rows + lax.broadcasted_iota(jnp.int32, (rows, 1), 0)
            weight = jnp.where(ids < own, prop[at, :], 0.0)
            part = weight * vertex[at, :].astype(jnp.float32)
            scaled[at, :] = jnp.where(col_ids < own, part, 0.0).astype(jnp.bfloat16)
            return carry

        lax.fori_loop(0, width // rows, fill, 0)

    at = pl.ds(pl.multiple_of(step * rows, rows), rows)
    product = jnp.dot(bare[...], scaled[...], preferred_element_type=jnp.float32)
    total = vertex[at, :].astype(jnp.float32) + product
    live = (step * rows + row_ids[:rows] < own) & (col_ids < own)
    base[...] = jnp.where(live, total, 0.0)


def ladder_base(order, bare, vertex, prop):
    width = vertex.shape[0]
    rows = min(256, width)
    whole = pl.BlockSpec((width, width), lambda i: (0, 0))
    return pl.pallas_call(
        ladder_body,
        grid=(width // rows,),
        out_shape=pltpu.HBM((width, width), jnp.float32),
        in_specs=[
            pl.BlockSpec(memory_space=pltpu.SMEM),
            pl.BlockSpec((rows, width), lambda i: (i, 0)),
            whole,
            pl.BlockSpec((width, 1), lambda i: (0, 0)),
        ],
        out_specs=pl.BlockSpec((rows, width), lambda i: (i, 0)),
        scratch_shapes=[pltpu.VMEM((width, width), jnp.bfloat16)],
        compiler_params=pltpu.CompilerParams(vmem_limit_bytes=GRANT),
        cost_estimate=pl.CostEstimate(
            flops=2 * width**3, bytes_accessed=8 * width * width, transcendentals=0
        ),
    )(order, bare, vertex, prop)


def exchange(tiles):
    return lax.all_to_all(tiles, AXES, split_axis=0, concat_axis=0, tiled=True)


def per_device(
    vertex, bare, pp_prop, ph_prop, orders, pandya_src, pandya_sixj, back_src, back_sixj
):
    per_owner, width, _ = vertex.shape
    parts = lax.axis_size(AXES)
    rows = width // parts
    assert per_owner == 1
    groups = digits()
    me = lax.axis_index(AXES).reshape(1)
    columns = small_columns(width)
    own_order = lax.dynamic_slice_in_dim(orders, me[0], 1)

    def recouple(small, large, src, sixj, masked):
        factors = jnp.swapaxes(sixj, 1, 2)
        small = small_exchange(small, groups)
        large = exchange(large)
        small = recouple_tiles(me, small, src, factors, orders, masked, groups, 0)
        small = small_exchange(small, groups)
        large = recouple_tiles(me, large, src, factors, orders, masked, None, columns)
        large = exchange(large)
        return small, large

    tiles = vertex[0].reshape(parts, rows, width)
    small = pack_small(me, tiles, groups)
    large = pack_large(tiles)
    small, large = recouple(small, large, pandya_src, pandya_sixj, False)
    small, large = cycle_block(me, ph_prop, small, large, groups)
    small, large = recouple(small, large, back_src, back_sixj, True)
    prop = pp_prop.reshape(width, 1)
    base = ladder_base(own_order, bare[0], vertex[0], prop)
    return finish(me, base, small, large, groups)[None]


def solution(mesh):
    placed = (
        P(AXES, None, None),
        P(AXES, None, None),
        P(AXES, None),
        P(AXES, None),
        P(),
        P(),
        P(None, None, AXES),
        P(),
        P(None, None, AXES),
    )
    return jax.shard_map(
        per_device,
        mesh=mesh,
        in_specs=placed,
        out_specs=P(AXES, None, None),
        check_vma=False,
    )
```

```python
import functools
import math

import jax
import jax.numpy as jnp
from jax import lax
from jax.experimental import pallas as pl
from jax.experimental.pallas import tpu as pltpu
from jax.sharding import PartitionSpec as P


AXES = ("jown", "pown")
LEAST_ORDER = 512


GRANT = 20 * 2**20
SHARE = 4


def in_hbm(x):
    return pltpu.with_memory_space_constraint(x, pltpu.HBM)


def digits():
    low = lax.axis_size("pown").bit_length() - 1
    high = lax.axis_size("jown").bit_length() - 1
    assert 1 << low == lax.axis_size("pown") and 1 << high == lax.axis_size("jown")
    first = list(range(low))[-2:]
    last = [low] if high else []
    middle = [b for b in range(low + high) if b not in first + last]
    return [group for group in (first, middle, last) if group]


def place(tile, me, groups):
    relative = tile ^ me
    at = relative * 0
    for group in groups:
        for bit in reversed(group):
            at = at * 2 + ((relative >> bit) & 1)
    return at


def unplace(at, groups):
    relative = at * 0
    for group in reversed(groups):
        for bit in group:
            relative = relative | ((at & 1) << bit)
            at = at >> 1
    return relative


def mask_of(digit, group):
    return sum(((digit >> i) & 1) << bit for i, bit in enumerate(group))


def small_exchange(pieces, groups):
    total = len(pieces) * pieces[0].shape[0]
    sizes = [1 << len(group) for group in groups]
    tail = pieces[0].shape[1:]
    tiles = None
    for axis, group in enumerate(groups):
        got = []
        for digit in range(sizes[axis]):
            if axis:
                sent = lax.index_in_dim(tiles, digit, axis, keepdims=False)
            else:
                sent = pieces[digit].reshape(*sizes[1:], *tail)
            if digit:
                mask = mask_of(digit, group)
                pairs = [(d, d ^ mask) for d in range(total)]
                sent = lax.ppermute(sent, AXES, pairs)
            got.append(sent)
        tiles = jnp.stack(got, axis)
    return tiles.reshape(total, *tail)


def small_columns(width):
    return max(128, width // SHARE // 128 * 128)


def scatter(me, groups, pieces, write):
    for digit, piece in enumerate(pieces):
        first = mask_of(digit, groups[0])

        def one(q, carry, piece=piece, first=first):
            write(piece, q, (unplace(q, groups[1:]) | first) ^ me)
            return carry

        lax.fori_loop(0, piece.shape[0], one, 0, unroll=8)


def pieces_of(total, groups, tail):
    digits_of = 1 << len(groups[0])
    shape = (total // digits_of, *tail)
    block = pl.BlockSpec(shape, lambda i: (0,) * len(shape))
    return (pltpu.HBM(shape, jnp.bfloat16),) * digits_of, (block,) * digits_of


def pack_body(groups, me, block, *pieces):
    def write(piece, q, tile):
        piece[q] = block[tile]

    scatter(me[0], groups, pieces, write)


def pack_small(me, tiles, groups):
    total, rows, width = tiles.shape
    columns = small_columns(width)
    shapes, specs = pieces_of(total, groups, (rows, columns))
    return pl.pallas_call(
        functools.partial(pack_body, groups),
        grid=(1,),
        out_shape=shapes,
        in_specs=[
            pl.BlockSpec(memory_space=pltpu.SMEM),
            pl.BlockSpec((total, rows, columns), lambda i: (0, 0, 0)),
        ],
        out_specs=specs,
        compiler_params=pltpu.CompilerParams(vmem_limit_bytes=GRANT),
        cost_estimate=pl.CostEstimate(
            flops=0, bytes_accessed=4 * total * rows * columns, transcendentals=0
        ),
    )(me, in_hbm(tiles))


def pack_large_body(block, large):
    large[...] = block[:, :, block.shape[2] - large.shape[2] :]


def pack_large(tiles):
    total, rows, width = tiles.shape
    group = total // 2
    rest = width - small_columns(width)
    return pl.pallas_call(
        pack_large_body,
        grid=(total // group,),
        out_shape=pltpu.HBM((total, rows, rest), tiles.dtype),
        in_specs=[pl.BlockSpec((group, rows, width), lambda i: (i, 0, 0))],
        out_specs=pl.BlockSpec((group, rows, rest), lambda i: (i, 0, 0)),
        compiler_params=pltpu.CompilerParams(vmem_limit_bytes=GRANT),
        cost_estimate=pl.CostEstimate(
            flops=0, bytes_accessed=4 * total * rows * width, transcendentals=0
        ),
    )(in_hbm(tiles))


def recouple_body(masked, groups, left, src, orders, me, factors, tiles, *mixed):
    width = tiles.shape[2]
    rows = tiles.shape[1]
    terms = src.shape[1]
    lanes = 256 if width % 256 == 0 else 128
    row_ids = me[0] * rows + lax.broadcasted_iota(jnp.int32, (rows, 1), 0)

    def write(out, to, c):
        own = orders[c]
        weights = factors[c]
        picks, lives, scales = [], [], []
        for k in range(terms):
            pick = src[c, k]
            live = own if masked else jnp.minimum(own, orders[pick])
            weight = jnp.where(row_ids < live, weights[:, k : k + 1], 0.0)
            picks.append(place(pick, me[0], groups) if groups else pick)
            lives.append(live)
            scales.append(jnp.broadcast_to(weight, (rows, lanes)))
        for start in range(0, width, lanes):
            at = pl.ds(start, lanes)
            edge = left + start + lanes > LEAST_ORDER
            ids = left + start + lax.broadcasted_iota(jnp.int32, (1, lanes), 1)
            summed = None
            for k in range(terms):
                part = scales[k] * tiles[picks[k], :, at].astype(jnp.float32)
                if edge and not masked:
                    part = jnp.where(ids < lives[k], part, 0.0)
                summed = part if summed is None else summed + part
            if edge and masked:
                summed = jnp.where(ids < own, summed, 0.0)
            out[to, :, at] = summed.astype(jnp.bfloat16)

    if groups:
        scatter(me[0], groups, mixed, write)
        return
    group = mixed[0].shape[0]
    base = pl.program_id(0) * group

    def one(c, carry):
        write(mixed[0], c, base + c)
        return carry

    lax.fori_loop(0, group, one, 0, unroll=8)


def recouple_tiles(me, tiles, src, factors, orders, masked, groups, left):
    total, rows, width = tiles.shape
    if groups:
        group = total
        shapes, specs = pieces_of(total, groups, (rows, width))
    else:
        group = max(g for g in range(1, total // 2 + 1) if total % g == 0)
        shapes = pltpu.HBM((total, rows, width), jnp.bfloat16)
        specs = pl.BlockSpec((group, rows, width), lambda i: (i, 0, 0))
    smem = pl.BlockSpec(memory_space=pltpu.SMEM)
    vmem = pl.BlockSpec(memory_space=pltpu.VMEM)
    return pl.pallas_call(
        functools.partial(recouple_body, masked, groups, left),
        grid=(total // group,),
        out_shape=shapes,
        in_specs=[smem, smem, smem, vmem, vmem],
        out_specs=specs,
        compiler_params=pltpu.CompilerParams(vmem_limit_bytes=GRANT),
        cost_estimate=pl.CostEstimate(
            flops=8 * total * rows * width,
            bytes_accessed=4 * total * rows * width,
            transcendentals=0,
        ),
    )(src, orders, me, factors, tiles)


def assemble(groups, me, small, rows_of):
    total, rows, _ = small.shape

    def one(t, carry):
        at = pl.ds(pl.multiple_of(t * rows, rows), rows)
        rows_of[at, :] = small[place(t, me, groups)]
        return carry

    lax.fori_loop(0, total, one, 0, unroll=4)


def weigh(block, prop):
    return (block.astype(jnp.float32) * prop).astype(jnp.bfloat16)


def cycle_rows(at, prop, left, large, right):
    columns = left.shape[1]
    width = columns + large.shape[1]
    upper, lower = right
    weighted = weigh(left[at, :], prop[:, :columns])
    product = jnp.dot(weighted, upper, preferred_element_type=jnp.float32)
    weighted = weigh(large[at, :], prop[:, columns:])
    product += jnp.dot(weighted, lower, preferred_element_type=jnp.float32)
    return (product * (1.0 / math.sqrt(width))).astype(jnp.bfloat16)


def cycle_small_body(groups, me, prop, small, large, *rest):
    pieces, (left, kept) = rest[:-2], rest[-2:]
    columns = small.shape[2]
    width = left.shape[0]
    height = min(256, width)
    assemble(groups, me[0], small, left)

    def one(step, carry):
        at = pl.ds(pl.multiple_of(step * height, height), height)
        right = (left[:columns, :], left[columns:, :])
        kept[at, :] = cycle_rows(at, prop, left, large, right)
        return carry

    lax.fori_loop(0, width // height, one, 0, unroll=True)
    rows = small.shape[1]

    def write(piece, q, tile):
        piece[q] = kept[pl.ds(pl.multiple_of(tile * rows, rows), rows), :]

    scatter(me[0], groups, pieces, write)


def cycle_small(me, prop, small, large, groups):
    total, rows, columns = small.shape
    width = total * rows
    vmem = pl.BlockSpec(memory_space=pltpu.VMEM)
    shapes, specs = pieces_of(total, groups, (rows, columns))
    return pl.pallas_call(
        functools.partial(cycle_small_body, groups),
        grid=(1,),
        out_shape=shapes,
        in_specs=[pl.BlockSpec(memory_space=pltpu.SMEM), vmem, vmem, vmem],
        out_specs=specs,
        scratch_shapes=[pltpu.VMEM((width, columns), jnp.bfloat16)] * 2,
        compiler_params=pltpu.CompilerParams(vmem_limit_bytes=GRANT),
        cost_estimate=pl.CostEstimate(
            flops=2 * width * width * columns,
            bytes_accessed=4 * width * width,
            transcendentals=0,
        ),
    )(me, prop, small, large.reshape(width, width - columns))


def cycle_large_body(groups, me, prop, small, large, out, left):
    step = pl.program_id(0)
    columns = small.shape[2]
    pl.when(step == 0)(lambda: assemble(groups, me[0], small, left))
    height = out.shape[0]
    at = pl.ds(pl.multiple_of(step * height, height), height)
    right = (large[:columns, :], large[columns:, :])
    out[...] = cycle_rows(at, prop, left, large, right)


def cycle_large(me, prop, small, large, groups):
    total, rows, columns = small.shape
    width = total * rows
    height = min(512, width)
    vmem = pl.BlockSpec(memory_space=pltpu.VMEM)
    cycle = pl.pallas_call(
        functools.partial(cycle_large_body, groups),
        grid=(width // height,),
        out_shape=pltpu.HBM((width, width - columns), jnp.bfloat16),
        in_specs=[pl.BlockSpec(memory_space=pltpu.SMEM), vmem, vmem, vmem],
        out_specs=pl.BlockSpec((height, width - columns), lambda i: (i, 0)),
        scratch_shapes=[pltpu.VMEM((width, columns), jnp.bfloat16)],
        compiler_params=pltpu.CompilerParams(vmem_limit_bytes=GRANT),
        cost_estimate=pl.CostEstimate(
            flops=2 * width * width * (width - columns),
            bytes_accessed=4 * width * width,
            transcendentals=0,
        ),
    )(me, prop, small, large.reshape(width, width - columns))
    return cycle.reshape(large.shape)


def finish_small_body(groups, me, base, small, updated):
    total, rows, _ = small.shape

    def one(t, carry):
        at = pl.ds(pl.multiple_of(t * rows, rows), rows)
        part = small[place(t, me[0], groups)].astype(jnp.float32)
        updated[at, :] = (base[at, :] + part).astype(jnp.bfloat16)
        return carry

    lax.fori_loop(0, total, one, 0, unroll=4)


def finish_small(me, base, small, groups):
    smem = pl.BlockSpec(memory_space=pltpu.SMEM)
    whole = pl.BlockSpec(base.shape, lambda i: (0, 0))
    return pl.pallas_call(
        functools.partial(finish_small_body, groups),
        grid=(1,),
        out_shape=pltpu.HBM(base.shape, jnp.bfloat16),
        in_specs=[smem, whole, pl.BlockSpec(small.shape, lambda i: (0, 0, 0))],
        out_specs=whole,
        compiler_params=pltpu.CompilerParams(vmem_limit_bytes=GRANT),
        cost_estimate=pl.CostEstimate(
            flops=2 * base.size, bytes_accessed=8 * base.size, transcendentals=0
        ),
    )(me, in_hbm(base), in_hbm(small))


def finish_body(done, base, large, updated):
    columns = done.shape[1]
    updated[:, :columns] = done[...]
    total = base[...] + large[...].astype(jnp.float32)
    updated[:, columns:] = total.astype(jnp.bfloat16)


def finish(done, base, large):
    width = base.shape[0]
    rows = width // 2

    def block(columns):
        return pl.BlockSpec((rows, columns), lambda i: (i, 0))

    return pl.pallas_call(
        finish_body,
        grid=(width // rows,),
        out_shape=pltpu.HBM((width, width), jnp.bfloat16),
        in_specs=[block(done.shape[1]), block(base.shape[1]), block(base.shape[1])],
        out_specs=block(width),
        compiler_params=pltpu.CompilerParams(vmem_limit_bytes=GRANT),
        cost_estimate=pl.CostEstimate(
            flops=2 * base.size, bytes_accessed=8 * base.size, transcendentals=0
        ),
    )(in_hbm(done), in_hbm(base), in_hbm(large.reshape(base.shape)))


def ladder_body(order, bare, vertex, prop, base, base_rest, scaled):
    rows, width = bare.shape
    step = pl.program_id(0)
    own = order[0]
    row_ids = lax.broadcasted_iota(jnp.int32, (width, 1), 0)
    col_ids = lax.broadcasted_iota(jnp.int32, (1, width), 1)

    @pl.when(step == 0)
    def _():
        def fill(i, carry):
            at = pl.ds(pl.multiple_of(i * rows, rows), rows)
            ids = i * rows + lax.broadcasted_iota(jnp.int32, (rows, 1), 0)
            weight = jnp.where(ids < own, prop[at, :], 0.0)
            part = weight * vertex[at, :].astype(jnp.float32)
            scaled[at, :] = jnp.where(col_ids < own, part, 0.0).astype(jnp.bfloat16)
            return carry

        lax.fori_loop(0, width // rows, fill, 0)

    at = pl.ds(pl.multiple_of(step * rows, rows), rows)
    product = jnp.dot(bare[...], scaled[...], preferred_element_type=jnp.float32)
    total = vertex[at, :].astype(jnp.float32) + product
    live = (step * rows + row_ids[:rows] < own) & (col_ids < own)
    total = jnp.where(live, total, 0.0)
    columns = base.shape[1]
    base[...] = total[:, :columns]
    base_rest[...] = total[:, columns:]


def ladder_base(order, bare, vertex, prop):
    width = vertex.shape[0]
    rows = min(256, width)
    columns = small_columns(width)
    whole = pl.BlockSpec((width, width), lambda i: (0, 0))
    return pl.pallas_call(
        ladder_body,
        grid=(width // rows,),
        out_shape=(
            pltpu.HBM((width, columns), jnp.float32),
            pltpu.HBM((width, width - columns), jnp.float32),
        ),
        in_specs=[
            pl.BlockSpec(memory_space=pltpu.SMEM),
            pl.BlockSpec((rows, width), lambda i: (i, 0)),
            whole,
            pl.BlockSpec((width, 1), lambda i: (0, 0)),
        ],
        out_specs=(
            pl.BlockSpec((rows, columns), lambda i: (i, 0)),
            pl.BlockSpec((rows, width - columns), lambda i: (i, 0)),
        ),
        scratch_shapes=[pltpu.VMEM((width, width), jnp.bfloat16)],
        compiler_params=pltpu.CompilerParams(vmem_limit_bytes=GRANT),
        cost_estimate=pl.CostEstimate(
            flops=2 * width**3, bytes_accessed=8 * width * width, transcendentals=0
        ),
    )(order, bare, vertex, prop)


def exchange(tiles):
    return lax.all_to_all(tiles, AXES, split_axis=0, concat_axis=0, tiled=True)


def per_device(
    vertex, bare, pp_prop, ph_prop, orders, pandya_src, pandya_sixj, back_src, back_sixj
):
    per_owner, width, _ = vertex.shape
    parts = lax.axis_size(AXES)
    rows = width // parts
    assert per_owner == 1
    groups = digits()
    me = lax.axis_index(AXES).reshape(1)
    columns = small_columns(width)
    own_order = lax.dynamic_slice_in_dim(orders, me[0], 1)

    def recouple(small, large, src, sixj, masked):
        factors = jnp.swapaxes(sixj, 1, 2)
        small = small_exchange(small, groups)
        large = exchange(large)
        small = recouple_tiles(me, small, src, factors, orders, masked, groups, 0)
        small = small_exchange(small, groups)
        large = recouple_tiles(me, large, src, factors, orders, masked, None, columns)
        large = exchange(large)
        return small, large

    tiles = vertex[0].reshape(parts, rows, width)
    small = pack_small(me, tiles, groups)
    large = pack_large(tiles)
    small, large = recouple(small, large, pandya_src, pandya_sixj, False)
    pieces = cycle_small(me, ph_prop, small, large, groups)
    small, large = pieces, cycle_large(me, ph_prop, small, large, groups)
    small, large = recouple(small, large, back_src, back_sixj, True)
    prop = pp_prop.reshape(width, 1)
    base, base_rest = ladder_base(own_order, bare[0], vertex[0], prop)
    done = finish_small(me, base, small, groups)
    return finish(done, base_rest, large)[None]


def solution(mesh):
    placed = (
        P(AXES, None, None),
        P(AXES, None, None),
        P(AXES, None),
        P(AXES, None),
        P(),
        P(),
        P(None, None, AXES),
        P(),
        P(None, None, AXES),
    )
    return jax.shard_map(
        per_device,
        mesh=mesh,
        in_specs=placed,
        out_specs=P(AXES, None, None),
        check_vma=False,
    )
```

```python
import functools
import math

import jax
import jax.numpy as jnp
from jax import lax
from jax.experimental import pallas as pl
from jax.experimental.pallas import tpu as pltpu
from jax.sharding import PartitionSpec as P


AXES = ("jown", "pown")
LEAST_ORDER = 512


GRANT = 20 * 2**20
SHARE = 4


def in_hbm(x):
    return pltpu.with_memory_space_constraint(x, pltpu.HBM)


def digits():
    low = lax.axis_size("pown").bit_length() - 1
    high = lax.axis_size("jown").bit_length() - 1
    assert 1 << low == lax.axis_size("pown") and 1 << high == lax.axis_size("jown")
    first = list(range(low))[-2:]
    last = [low] if high else []
    middle = [b for b in range(low + high) if b not in first + last]
    return [group for group in (first, middle, last) if group]


def place(tile, me, groups):
    relative = tile ^ me
    at = relative * 0
    for group in groups:
        for bit in reversed(group):
            at = at * 2 + ((relative >> bit) & 1)
    return at


def unplace(at, groups):
    relative = at * 0
    for group in reversed(groups):
        for bit in group:
            relative = relative | ((at & 1) << bit)
            at = at >> 1
    return relative


def mask_of(digit, group):
    return sum(((digit >> i) & 1) << bit for i, bit in enumerate(group))


def small_exchange(pieces, groups):
    total = len(pieces) * pieces[0].shape[0]
    sizes = [1 << len(group) for group in groups]
    tail = pieces[0].shape[1:]
    tiles = None
    for axis, group in enumerate(groups):
        got = []
        for digit in range(sizes[axis]):
            if axis:
                sent = lax.index_in_dim(tiles, digit, axis, keepdims=False)
            else:
                sent = pieces[digit].reshape(*sizes[1:], *tail)
            if digit:
                mask = mask_of(digit, group)
                pairs = [(d, d ^ mask) for d in range(total)]
                sent = lax.ppermute(sent, AXES, pairs)
            got.append(sent)
        tiles = jnp.stack(got, axis)
    return tiles.reshape(total, *tail)


def small_columns(width):
    return max(128, width // SHARE // 128 * 128)


def scatter(me, groups, pieces, write):
    for digit, piece in enumerate(pieces):
        first = mask_of(digit, groups[0])

        def one(q, carry, piece=piece, first=first):
            write(piece, q, (unplace(q, groups[1:]) | first) ^ me)
            return carry

        lax.fori_loop(0, piece.shape[0], one, 0, unroll=8)


def pieces_of(total, groups, tail):
    digits_of = 1 << len(groups[0])
    shape = (total // digits_of, *tail)
    block = pl.BlockSpec(shape, lambda i: (0,) * len(shape))
    return (pltpu.HBM(shape, jnp.bfloat16),) * digits_of, (block,) * digits_of


def pack_body(groups, me, block, *pieces):
    def write(piece, q, tile):
        piece[q] = block[tile]

    scatter(me[0], groups, pieces, write)


def pack_small(me, tiles, groups):
    total, rows, width = tiles.shape
    columns = small_columns(width)
    shapes, specs = pieces_of(total, groups, (rows, columns))
    return pl.pallas_call(
        functools.partial(pack_body, groups),
        grid=(1,),
        out_shape=shapes,
        in_specs=[
            pl.BlockSpec(memory_space=pltpu.SMEM),
            pl.BlockSpec((total, rows, columns), lambda i: (0, 0, 0)),
        ],
        out_specs=specs,
        compiler_params=pltpu.CompilerParams(vmem_limit_bytes=GRANT),
        cost_estimate=pl.CostEstimate(
            flops=0, bytes_accessed=4 * total * rows * columns, transcendentals=0
        ),
    )(me, in_hbm(tiles))


def pack_large_body(block, large):
    large[...] = block[:, :, block.shape[2] - large.shape[2] :]


def pack_large(tiles):
    total, rows, width = tiles.shape
    group = total // 2
    rest = width - small_columns(width)
    return pl.pallas_call(
        pack_large_body,
        grid=(total // group,),
        out_shape=pltpu.HBM((total, rows, rest), tiles.dtype),
        in_specs=[pl.BlockSpec((group, rows, width), lambda i: (i, 0, 0))],
        out_specs=pl.BlockSpec((group, rows, rest), lambda i: (i, 0, 0)),
        compiler_params=pltpu.CompilerParams(vmem_limit_bytes=GRANT),
        cost_estimate=pl.CostEstimate(
            flops=0, bytes_accessed=4 * total * rows * width, transcendentals=0
        ),
    )(in_hbm(tiles))


def recouple_body(masked, groups, left, src, orders, me, factors, tiles, *mixed):
    width = tiles.shape[2]
    rows = tiles.shape[1]
    terms = src.shape[1]
    lanes = 256 if width % 256 == 0 else 128
    row_ids = me[0] * rows + lax.broadcasted_iota(jnp.int32, (rows, 1), 0)

    def write(out, to, c):
        own = orders[c]
        weights = factors[c]
        picks, lives, scales = [], [], []
        for k in range(terms):
            pick = src[c, k]
            live = own if masked else jnp.minimum(own, orders[pick])
            weight = jnp.where(row_ids < live, weights[:, k : k + 1], 0.0)
            picks.append(place(pick, me[0], groups) if groups else pick)
            lives.append(live)
            scales.append(jnp.broadcast_to(weight, (rows, lanes)))
        for start in range(0, width, lanes):
            at = pl.ds(start, lanes)
            edge = left + start + lanes > LEAST_ORDER
            ids = left + start + lax.broadcasted_iota(jnp.int32, (1, lanes), 1)
            summed = None
            for k in range(terms):
                part = scales[k] * tiles[picks[k], :, at].astype(jnp.float32)
                if edge and not masked:
                    part = jnp.where(ids < lives[k], part, 0.0)
                summed = part if summed is None else summed + part
            if edge and masked:
                summed = jnp.where(ids < own, summed, 0.0)
            out[to, :, at] = summed.astype(jnp.bfloat16)

    if groups:
        scatter(me[0], groups, mixed, write)
        return
    group = mixed[0].shape[0]
    base = pl.program_id(0) * group

    def one(c, carry):
        write(mixed[0], c, base + c)
        return carry

    lax.fori_loop(0, group, one, 0, unroll=8)


def recouple_tiles(me, tiles, src, factors, orders, masked, groups, left):
    total, rows, width = tiles.shape
    if groups:
        group = total
        shapes, specs = pieces_of(total, groups, (rows, width))
    else:
        group = max(g for g in range(1, total // 2 + 1) if total % g == 0)
        shapes = pltpu.HBM((total, rows, width), jnp.bfloat16)
        specs = pl.BlockSpec((group, rows, width), lambda i: (i, 0, 0))
    smem = pl.BlockSpec(memory_space=pltpu.SMEM)
    vmem = pl.BlockSpec(memory_space=pltpu.VMEM)
    return pl.pallas_call(
        functools.partial(recouple_body, masked, groups, left),
        grid=(total // group,),
        out_shape=shapes,
        in_specs=[smem, smem, smem, vmem, vmem],
        out_specs=specs,
        compiler_params=pltpu.CompilerParams(vmem_limit_bytes=GRANT),
        cost_estimate=pl.CostEstimate(
            flops=8 * total * rows * width,
            bytes_accessed=4 * total * rows * width,
            transcendentals=0,
        ),
    )(src, orders, me, factors, tiles)


def assemble(groups, me, small, rows_of):
    total, rows, _ = small.shape

    def one(t, carry):
        at = pl.ds(pl.multiple_of(t * rows, rows), rows)
        rows_of[at, :] = small[place(t, me, groups)]
        return carry

    lax.fori_loop(0, total, one, 0, unroll=4)


def weigh(block, prop):
    return (block.astype(jnp.float32) * prop).astype(jnp.bfloat16)


def cycle_rows(at, prop, left, large, right):
    columns = left.shape[1]
    width = columns + large.shape[1]
    upper, lower = right
    weighted = weigh(left[at, :], prop[:, :columns])
    product = jnp.dot(weighted, upper, preferred_element_type=jnp.float32)
    weighted = weigh(large[at, :], prop[:, columns:])
    product += jnp.dot(weighted, lower, preferred_element_type=jnp.float32)
    return (product * (1.0 / math.sqrt(width))).astype(jnp.bfloat16)


def cycle_small_body(groups, me, prop, small, large, *rest):
    pieces, (left, kept) = rest[:-2], rest[-2:]
    columns = small.shape[2]
    width = left.shape[0]
    height = min(512, width)
    assemble(groups, me[0], small, left)

    def one(step, carry):
        at = pl.ds(pl.multiple_of(step * height, height), height)
        right = (left[:columns, :], left[columns:, :])
        kept[at, :] = cycle_rows(at, prop, left, large, right)
        return carry

    lax.fori_loop(0, width // height, one, 0, unroll=True)
    rows = small.shape[1]

    def write(piece, q, tile):
        piece[q] = kept[pl.ds(pl.multiple_of(tile * rows, rows), rows), :]

    scatter(me[0], groups, pieces, write)


def cycle_small(me, prop, small, large, groups):
    total, rows, columns = small.shape
    width = total * rows
    vmem = pl.BlockSpec(memory_space=pltpu.VMEM)
    shapes, specs = pieces_of(total, groups, (rows, columns))
    return pl.pallas_call(
        functools.partial(cycle_small_body, groups),
        grid=(1,),
        out_shape=shapes,
        in_specs=[pl.BlockSpec(memory_space=pltpu.SMEM), vmem, vmem, vmem],
        out_specs=specs,
        scratch_shapes=[pltpu.VMEM((width, columns), jnp.bfloat16)] * 2,
        compiler_params=pltpu.CompilerParams(vmem_limit_bytes=GRANT),
        cost_estimate=pl.CostEstimate(
            flops=2 * width * width * columns,
            bytes_accessed=4 * width * width,
            transcendentals=0,
        ),
    )(me, prop, small, large.reshape(width, width - columns))


def cycle_large_body(groups, me, prop, small, large, out, left):
    step = pl.program_id(0)
    columns = small.shape[2]
    pl.when(step == 0)(lambda: assemble(groups, me[0], small, left))
    height = out.shape[0]
    at = pl.ds(pl.multiple_of(step * height, height), height)
    right = (large[:columns, :], large[columns:, :])
    out[...] = cycle_rows(at, prop, left, large, right)


def cycle_large(me, prop, small, large, groups):
    total, rows, columns = small.shape
    width = total * rows
    height = min(512, width)
    vmem = pl.BlockSpec(memory_space=pltpu.VMEM)
    cycle = pl.pallas_call(
        functools.partial(cycle_large_body, groups),
        grid=(width // height,),
        out_shape=pltpu.HBM((width, width - columns), jnp.bfloat16),
        in_specs=[pl.BlockSpec(memory_space=pltpu.SMEM), vmem, vmem, vmem],
        out_specs=pl.BlockSpec((height, width - columns), lambda i: (i, 0)),
        scratch_shapes=[pltpu.VMEM((width, columns), jnp.bfloat16)],
        compiler_params=pltpu.CompilerParams(vmem_limit_bytes=GRANT),
        cost_estimate=pl.CostEstimate(
            flops=2 * width * width * (width - columns),
            bytes_accessed=4 * width * width,
            transcendentals=0,
        ),
    )(me, prop, small, large.reshape(width, width - columns))
    return cycle.reshape(large.shape)


def finish_body(groups, me, base, small, large, updated):
    step = pl.program_id(0)
    group, rows, _ = large.shape
    columns = small.shape[2]

    def one(t, carry):
        at = pl.ds(pl.multiple_of(t * rows, rows), rows)
        part = small[place(step * group + t, me[0], groups)].astype(jnp.float32)
        updated[at, :columns] = (base[at, :columns] + part).astype(jnp.bfloat16)
        part = large[t].astype(jnp.float32)
        updated[at, columns:] = (base[at, columns:] + part).astype(jnp.bfloat16)
        return carry

    lax.fori_loop(0, group, one, 0, unroll=4)


def finish(me, base, small, large, groups):
    total, rows, columns = small.shape
    width = base.shape[1]
    group = total // 2
    block = pl.BlockSpec((group * rows, width), lambda i: (i, 0))
    return pl.pallas_call(
        functools.partial(finish_body, groups),
        grid=(total // group,),
        out_shape=pltpu.HBM(base.shape, jnp.bfloat16),
        in_specs=[
            pl.BlockSpec(memory_space=pltpu.SMEM),
            block,
            pl.BlockSpec(memory_space=pltpu.VMEM),
            pl.BlockSpec((group, rows, width - columns), lambda i: (i, 0, 0)),
        ],
        out_specs=block,
        compiler_params=pltpu.CompilerParams(vmem_limit_bytes=GRANT),
        cost_estimate=pl.CostEstimate(
            flops=2 * base.size, bytes_accessed=8 * base.size, transcendentals=0
        ),
    )(me, in_hbm(base), small, in_hbm(large))


def ladder_body(order, bare, vertex, prop, base, scaled):
    rows, width = bare.shape
    step = pl.program_id(0)
    own = order[0]
    row_ids = lax.broadcasted_iota(jnp.int32, (width, 1), 0)
    col_ids = lax.broadcasted_iota(jnp.int32, (1, width), 1)

    @pl.when(step == 0)
    def _():
        def fill(i, carry):
            at = pl.ds(pl.multiple_of(i * rows, rows), rows)
            ids = i * rows + lax.broadcasted_iota(jnp.int32, (rows, 1), 0)
            weight = jnp.where(ids < own, prop[at, :], 0.0)
            part = weight * vertex[at, :].astype(jnp.float32)
            scaled[at, :] = jnp.where(col_ids < own, part, 0.0).astype(jnp.bfloat16)
            return carry

        lax.fori_loop(0, width // rows, fill, 0)

    at = pl.ds(pl.multiple_of(step * rows, rows), rows)
    product = jnp.dot(bare[...], scaled[...], preferred_element_type=jnp.float32)
    total = vertex[at, :].astype(jnp.float32) + product
    live = (step * rows + row_ids[:rows] < own) & (col_ids < own)
    base[...] = jnp.where(live, total, 0.0)


def ladder_base(order, bare, vertex, prop):
    width = vertex.shape[0]
    rows = min(256, width)
    whole = pl.BlockSpec((width, width), lambda i: (0, 0))
    return pl.pallas_call(
        ladder_body,
        grid=(width // rows,),
        out_shape=pltpu.HBM((width, width), jnp.float32),
        in_specs=[
            pl.BlockSpec(memory_space=pltpu.SMEM),
            pl.BlockSpec((rows, width), lambda i: (i, 0)),
            whole,
            pl.BlockSpec((width, 1), lambda i: (0, 0)),
        ],
        out_specs=pl.BlockSpec((rows, width), lambda i: (i, 0)),
        scratch_shapes=[pltpu.VMEM((width, width), jnp.bfloat16)],
        compiler_params=pltpu.CompilerParams(vmem_limit_bytes=GRANT),
        cost_estimate=pl.CostEstimate(
            flops=2 * width**3, bytes_accessed=8 * width * width, transcendentals=0
        ),
    )(order, bare, vertex, prop)


def exchange(tiles):
    return lax.all_to_all(tiles, AXES, split_axis=0, concat_axis=0, tiled=True)


def per_device(
    vertex, bare, pp_prop, ph_prop, orders, pandya_src, pandya_sixj, back_src, back_sixj
):
    per_owner, width, _ = vertex.shape
    parts = lax.axis_size(AXES)
    rows = width // parts
    assert per_owner == 1
    groups = digits()
    me = lax.axis_index(AXES).reshape(1)
    columns = small_columns(width)
    own_order = lax.dynamic_slice_in_dim(orders, me[0], 1)

    def recouple(small, large, src, sixj, masked):
        factors = jnp.swapaxes(sixj, 1, 2)
        small = small_exchange(small, groups)
        large = exchange(large)
        small = recouple_tiles(me, small, src, factors, orders, masked, groups, 0)
        small = small_exchange(small, groups)
        large = recouple_tiles(me, large, src, factors, orders, masked, None, columns)
        large = exchange(large)
        return small, large

    tiles = vertex[0].reshape(parts, rows, width)
    small = pack_small(me, tiles, groups)
    large = pack_large(tiles)
    small, large = recouple(small, large, pandya_src, pandya_sixj, False)
    pieces = cycle_small(me, ph_prop, small, large, groups)
    small, large = pieces, cycle_large(me, ph_prop, small, large, groups)
    small, large = recouple(small, large, back_src, back_sixj, True)
    prop = pp_prop.reshape(width, 1)
    base = ladder_base(own_order, bare[0], vertex[0], prop)
    return finish(me, base, small, large, groups)[None]


def solution(mesh):
    placed = (
        P(AXES, None, None),
        P(AXES, None, None),
        P(AXES, None),
        P(AXES, None),
        P(),
        P(),
        P(None, None, AXES),
        P(),
        P(None, None, AXES),
    )
    return jax.shard_map(
        per_device,
        mesh=mesh,
        in_specs=placed,
        out_specs=P(AXES, None, None),
        check_vma=False,
    )
```
